32 devices in a mesh: dp: 4 (over y, x), ctx: 8 (over z, core).
Axes of the slice: x: 2, y: 2, z: 4, core: 2. Of those that a mesh axis runs over, the one named last changes fastest.
Arguments:
- tokens: bfloat16 [4096, 2048], P('ctx', 'dp'), may hold values from -6 to 6
- input_gain: float32 [2048], replicated, may hold values from 0.1 to 1.9
- projections: bfloat16 [3, 2048, 1024], P(None, 'dp'), may hold values from -0.125 to 0.125
- head_gain: float32 [1024], P('dp'), may hold values from 0.1 to 1.9
Outputs:
- attended: bfloat16 [4096, 1024], P('ctx', 'dp')
The draws below stay inside these ranges and needn't reach their ends.
All inputs are finite; a program needn't handle non-finite values.
Results may differ from the reference program's by a relative error of at most 0.0061.
Values may be sent and summed in bfloat16 or wider, within the bound.
No kernel may reach another device: no remote copies, remote signals or barrier semaphores. Data moves between devices by JAX's collectives and lax.ppermute only.
A program may use at most 64 MiB of HBM per device.

```python
import jax
import jax.numpy as jnp
from jax import lax

D = 2048
HEADS = 8
HEAD_DIM = 128
TOK_DEV = 512
HE = 1024
LENGTH = 4096
N_CTX = 8


def levels(stream_key, shape, cuts, smallest, high):
    level, own = 1.0, jax.random.fold_in(stream_key, 6)
    for axis_at, parts in cuts:
        steps = jnp.exp(jax.random.uniform(jax.random.fold_in(own, axis_at), (parts,), jnp.float32, smallest / len(cuts), high / len(cuts)))
        level = level * jnp.repeat(steps, shape[axis_at] // parts).reshape([-1 if axis == axis_at else 1 for axis in range(len(shape))])
    return level


def noise(rng, extent, width, reach, split=(), kind=jnp.bfloat16):
    gain = levels(rng, extent, split, -0.22, 0.18) if split else 1.0
    result = jax.random.normal(rng, extent, jnp.float32) * width * gain
    return jnp.minimum(jnp.maximum(result, -reach), reach).astype(kind)


def setup_inputs(seed: int = 0) -> dict:
    keys = jax.random.split(jax.random.key(seed), 5)
    tokens = noise(keys[0], (LENGTH, D), 1.0, 6.0, ((0, 8), (1, 4)))
    input_gain = jnp.clip(1.0 + 0.18 * jax.random.normal(keys[1], (D,), jnp.float32), 0.1, 1.9)
    projections = noise(keys[2], (3, D, HE), D ** -0.5, 0.125, ((1, 4),))
    head_gain = jnp.clip(1.0 + 0.18 * jax.random.normal(keys[3], (HE,), jnp.float32), 0.1, 1.9)
    return dict(tokens=tokens, input_gain=input_gain, projections=projections, head_gain=head_gain)


epsilon = 1e-05

def feature(inputs):
    return jnp.where(inputs > 0, inputs + 1.0, jnp.exp(jnp.minimum(inputs, 0.0)))

def rounded(inputs):
    return lax.optimization_barrier(inputs.astype(jnp.bfloat16)).astype(jnp.float32)

def reference(tokens, input_gain, projections, head_gain):
    weights = projections.astype(jnp.float32)
    gains = head_gain.reshape(HEADS, HEAD_DIM)
    rows = jnp.arange(TOK_DEV, dtype=jnp.int32)
    causal = rows[:, None] >= rows[None, :]
    inputs = tokens.astype(jnp.float32)
    scale = lax.rsqrt(lax.optimization_barrier(jnp.mean(inputs * inputs, axis=-1, keepdims=True)) + epsilon)
    normed = rounded(inputs * scale * input_gain)
    shape = (N_CTX, TOK_DEV, HEADS, HEAD_DIM)
    queries = rounded(feature(jnp.dot(normed, weights[0]))).reshape(shape)
    key_feats = rounded(feature(jnp.dot(normed, weights[1]))).reshape(shape)
    values = rounded(jnp.dot(normed, weights[2])).reshape(shape)
    local_state = jnp.einsum('nthe,nthf->nhef', key_feats, values)
    running = jnp.cumsum(local_state, axis=0)
    prior = jnp.concatenate([jnp.zeros_like(local_state[:1]), running[:-1]], axis=0)
    prior_state = rounded(prior)

    def one_block(pieces):
        query_block, key_block, value_block, state_block = pieces
        scores = jnp.einsum('the,she->hts', query_block, key_block)
        scores = rounded(jnp.where(causal[None], scores, 0.0))
        inner = jnp.einsum('hts,shf->thf', scores, value_block)
        outer = jnp.einsum('the,hef->thf', query_block, state_block)
        mixed_out = inner + outer
        factor = lax.rsqrt(lax.optimization_barrier(jnp.mean(mixed_out * mixed_out, axis=-1, keepdims=True)) + epsilon)
        return (mixed_out * factor * gains).astype(jnp.bfloat16)
    attended = lax.map(one_block, (queries, key_feats, values, prior_state))
    return attended.reshape(LENGTH, HEADS * HEAD_DIM)
```

```python
import jax
import jax.numpy as jnp
from jax import lax
from jax.experimental import pallas as pl
from jax.experimental.pallas import tpu as pltpu
from jax.sharding import PartitionSpec as P

HEAD_DIM = 128
epsilon = 1e-05
F32 = jnp.float32
BF16 = jnp.bfloat16
Q, K, V = 0, 1, 2


def feature(inputs):
    return jnp.where(inputs > 0, inputs + 1.0, jnp.exp(jnp.minimum(inputs, 0.0)))


def mm(a, b):
    return jnp.dot(a, b, preferred_element_type=F32)


def gained(x_ref, g_ref):
    return (x_ref[...].astype(F32) * g_ref[...]).astype(BF16)


def xor_pairs(size, bits):
    return [(i, i ^ bits) for i in range(size)]


def body(tokens, input_gain, projections, head_gain):
    steps, features = tokens.shape
    width = head_gain.shape[0]
    n_dp = lax.axis_size("dp")
    n_ctx = lax.axis_size("ctx")
    heads = width // HEAD_DIM
    total = features * n_dp
    assert n_dp == 4 and heads == 2 and n_ctx % 2 == 0
    H = HEAD_DIM
    mine = lax.axis_index("dp").astype(jnp.int32)
    where = jnp.full((1,), mine, jnp.int32)
    gain = input_gain.reshape(1, total)

    x_spec = pl.BlockSpec((steps, features), lambda i, m: (0, 0))
    g_spec = pl.BlockSpec((1, features), lambda i, m: (0, m[0]))

    def w_slot(matrix, bits, slot):
        return pl.BlockSpec((None, features, H), lambda i, m: (matrix, 0, (m[0] ^ bits) * 2 + slot))

    def w_both(matrix, bits):
        return pl.BlockSpec((None, features, width), lambda i, m: (matrix, 0, m[0] ^ bits))

    def cols(n, at=0):
        return pl.BlockSpec((steps, n), lambda i, m: (0, at))

    def call(kernel, name, ins, outs, flops):
        specs = [s for s, _ in ins]
        arrays = [a for _, a in ins]
        moved = sum(a.size * a.dtype.itemsize for s, a in ins if a is not projections)
        moved += sum(s.size * s.dtype.itemsize for s in outs)
        return pl.pallas_call(
            kernel,
            name=name,
            grid_spec=pltpu.PrefetchScalarGridSpec(
                num_scalar_prefetch=1,
                grid=(1,),
                in_specs=specs,
                out_specs=[pl.BlockSpec(o.shape, lambda i, m, r=len(o.shape): (0,) * r) for o in outs],
            ),
            out_shape=outs,
            cost_estimate=pl.CostEstimate(flops=flops, bytes_accessed=moved, transcendentals=0),
        )(where, *arrays)

    def arr(*shape, dtype=BF16):
        return jax.ShapeDtypeStruct(shape, dtype)

    base = [(x_spec, tokens), (g_spec, gain)]
    block = 2 * steps * features * H

    def w(spec):
        return (spec, projections)

    def first_kernel(m, x, g, w01, w03, w12, w13, o0, o1):
        xg = gained(x, g)
        o0[:, :H] = mm(xg, w01[...]).astype(BF16)
        o0[:, H:] = mm(xg, w03[...]).astype(BF16)
        o1[:, :H] = mm(xg, w12[...]).astype(BF16)
        o1[:, H:] = mm(xg, w13[...]).astype(BF16)

    def first(matrix, name):
        ins = base + [w(w_slot(matrix, 1, 0)), w(w_slot(matrix, 3, 0)), w(w_slot(matrix, 2, 1)), w(w_slot(matrix, 3, 1))]
        s0, s1 = call(first_kernel, name, ins, [arr(steps, 2 * H)] * 2, 4 * block)
        return lax.ppermute(s0, "dp", xor_pairs(n_dp, 1)), lax.ppermute(s1, "dp", xor_pairs(n_dp, 2))

    k1 = first(K, "first_k")
    v1 = first(V, "first_v")

    def squares_kernel(m, x, o):
        xf = x[...].astype(F32)
        sq = xf * xf
        hi = sq.astype(BF16)
        lo = (sq - hi.astype(F32)).astype(BF16)
        ones = jnp.ones((8, features), BF16)
        dims = (((1,), (1,)), ((), ()))
        o[...] = lax.dot_general(ones, hi, dims, preferred_element_type=F32) + lax.dot_general(ones, lo, dims, preferred_element_type=F32)

    (sq,) = call(squares_kernel, "squares", base[:1], [arr(8, steps, dtype=F32)], block // 8)
    sq_others = [lax.ppermute(sq, "dp", xor_pairs(n_dp, b)) for b in (1, 2, 3)]

    def second_kernel(m, x, g, w02, w11, r0, r1, o0, o1):
        xg = gained(x, g)
        o0[...] = (mm(xg, w02[...]) + r0[...].astype(F32)).astype(BF16)
        o1[...] = (mm(xg, w11[...]) + r1[...].astype(F32)).astype(BF16)

    def second(matrix, received, name):
        ins = base + [w(w_slot(matrix, 2, 0)), w(w_slot(matrix, 1, 1)), (cols(H, 1), received[0]), (cols(H, 1), received[1])]
        s0, s1 = call(second_kernel, name, ins, [arr(steps, H)] * 2, 2 * block)
        return lax.ppermute(s0, "dp", xor_pairs(n_dp, 2)), lax.ppermute(s1, "dp", xor_pairs(n_dp, 1))

    k2 = second(K, k1, "second_k")
    v2 = second(V, v1, "second_v")

    def query_kernel(m, x, g, w1, w2, w3, o1, o2, o3):
        xg = gained(x, g)
        for wr, o in ((w1, o1), (w2, o2), (w3, o3)):
            o[...] = mm(xg, wr[...]).astype(BF16)

    ins = base + [w(w_both(Q, b)) for b in (1, 2, 3)]
    sends = call(query_kernel, "query", ins, [arr(steps, width)] * 3, 6 * block)
    q_others = [lax.ppermute(s, "dp", xor_pairs(n_dp, b)) for b, s in zip((1, 2, 3), sends)]

    row = pl.BlockSpec((8, steps), lambda i, m: (0, 0))
    scale_spec = cols(H)

    def keys_kernel(m, x, g, wk, wv, s0, s1, s2, s3, ka0, ka1, kb0, kb1, va0, va1, o_k, o_v, o_s):
        ss = s0[...] + s1[...] + s2[...] + s3[...]
        inv = lax.rsqrt(ss * (1.0 / total) + epsilon)
        scale = jnp.broadcast_to(inv[:1, :], (H, steps)).T
        o_s[...] = scale
        xg = gained(x, g)
        own = mm(xg, wk[...])
        for h, (a, b) in enumerate(((ka0, kb0), (ka1, kb1))):
            at = slice(h * H, h * H + H)
            u = (own[:, at] + a[...].astype(F32) + b[...].astype(F32)) * scale
            o_k[:, at] = feature(u).astype(BF16)
        own = mm(xg, wv[...])
        for h, a in enumerate((va0, va1)):
            at = slice(h * H, h * H + H)
            o_v[:, at] = own[:, at] + a[...].astype(F32)

    ins = base + [w(w_both(K, 0)), w(w_both(V, 0)), (row, sq)] + [(row, s) for s in sq_others]
    ins += [(cols(H), k1[0]), (cols(H), k1[1]), (cols(H), k2[0]), (cols(H), k2[1]), (cols(H), v1[0]), (cols(H), v1[1])]
    outs = [arr(steps, width), arr(steps, width, dtype=F32), arr(steps, H, dtype=F32)]
    keys, v_own, scale = call(keys_kernel, "keys", ins, outs, 4 * block)

    def values_kernel(m, k, v, s, b0, b1, o_v, o_st):
        for h, b in enumerate((b0, b1)):
            at = slice(h * H, h * H + H)
            val = ((v[:, at] + b[...].astype(F32)) * s[...]).astype(BF16)
            o_v[:, at] = val
            o_st[h] = lax.dot_general(k[:, at], val, (((0,), (0,)), ((), ())), preferred_element_type=F32)

    ins = [(cols(width), keys), (cols(width), v_own), (scale_spec, scale), (cols(H), v2[0]), (cols(H), v2[1])]
    outs = [arr(steps, width), arr(heads, H, H, dtype=F32)]
    values, state = call(values_kernel, "values", ins, outs, 4 * steps * H * H)

    prior = entering(state, n_ctx)

    def query_act(m, x, g, wq, s, r1, r2, r3, at, xg):
        own = mm(xg, wq[:, at])
        u = own + r1[:, at].astype(F32) + r2[:, at].astype(F32) + r3[:, at].astype(F32)
        return feature(u * s[...]).astype(BF16)

    def inner_kernel(m, x, g, wq, s, r1, r2, r3, k, v, o_q, o_m):
        xg = gained(x, g)
        rows = lax.broadcasted_iota(jnp.int32, (steps, steps), 0)
        columns = lax.broadcasted_iota(jnp.int32, (steps, steps), 1)
        causal = rows >= columns
        for h in range(heads):
            at = slice(h * H, h * H + H)
            q = query_act(m, x, g, wq, s, r1, r2, r3, at, xg)
            o_q[:, at] = q
            sc = lax.dot_general(q, k[:, at], (((1,), (1,)), ((), ())), preferred_element_type=F32)
            sc = jnp.where(causal, sc, 0.0).astype(BF16)
            o_m[:, at] = mm(sc, v[:, at])

    ins = base + [w(w_both(Q, 0)), (scale_spec, scale)] + [(cols(width), r) for r in q_others] + [(cols(width), keys), (cols(width), values)]
    outs = [arr(steps, width), arr(steps, width, dtype=F32)]
    queries, inner = call(inner_kernel, "inner", ins, outs, 2 * block + 8 * steps * steps * H)

    def outer_kernel(m, q, inner, st, hg, o):
        for h in range(heads):
            at = slice(h * H, h * H + H)
            mixed = inner[:, at] + mm(q[:, at], st[h])
            factor = lax.rsqrt(jnp.mean(mixed * mixed, axis=-1, keepdims=True) + epsilon)
            o[:, at] = (mixed * factor * hg[:, at]).astype(BF16)

    st_spec = pl.BlockSpec((heads, H, H), lambda i, m: (0, 0, 0))
    hg_spec = pl.BlockSpec((1, width), lambda i, m: (0, 0))
    ins = [(cols(width), queries), (cols(width), inner), (st_spec, prior), (hg_spec, head_gain.reshape(1, width))]
    (out,) = call(outer_kernel, "outer", ins, [arr(steps, width)], 4 * steps * H * H)
    return out


def entering(state, n_ctx):
    at = lax.axis_index("ctx")
    odd = (at & 1) == 1
    own = jnp.where(odd, state[1], state[0])
    give = jnp.where(odd, state[0], state[1]).astype(BF16)
    partner = lax.ppermute(give, "ctx", xor_pairs(n_ctx, 1)).astype(F32)
    group = own + partner
    before = jnp.zeros_like(own)
    chips, span = n_ctx // 2, 1
    while span < chips:
        radix = 4 if chips % (span * 4) == 0 else 2
        digit = (at // (2 * span)) % radix
        sent = group.astype(BF16)
        for bits in range(1, radix):
            came = lax.ppermute(sent, "ctx", xor_pairs(n_ctx, 2 * span * bits)).astype(F32)
            before = before + jnp.where((digit ^ bits) < digit, came, 0.0)
            group = group + came
        span *= radix
    assert span == chips
    theirs = before + jnp.where(odd, 0.0, own)
    ours = (before + jnp.where(odd, partner, 0.0)).astype(BF16)
    other = lax.ppermute(theirs.astype(BF16), "ctx", xor_pairs(n_ctx, 1))
    return jnp.stack([jnp.where(odd, other, ours), jnp.where(odd, ours, other)])


def solution(mesh):
    in_specs = (P("ctx", "dp"), P(), P(None, "dp", None), P("dp"))
    out_specs = P("ctx", "dp")
    return jax.shard_map(body, mesh=mesh, in_specs=in_specs, out_specs=out_specs, check_vma=False)
```

```python
import jax
import jax.numpy as jnp
from jax import lax
from jax.experimental import pallas as pl
from jax.experimental.pallas import tpu as pltpu
from jax.sharding import PartitionSpec as P

HEAD_DIM = 128
epsilon = 1e-05
F32 = jnp.float32
BF16 = jnp.bfloat16
Q, K, V = 0, 1, 2
VMEM_LIMIT = 8 * 2**20


def feature(inputs):
    return jnp.where(inputs > 0, inputs + 1.0, jnp.exp(jnp.minimum(inputs, 0.0)))


def mm(a, b):
    return jnp.dot(a, b, preferred_element_type=F32)


def swap(value, axis, bits):
    return lax.ppermute(value, axis, [(i, i ^ bits) for i in range(lax.axis_size(axis))])


def body(tokens, input_gain, projections, head_gain):
    steps, features = tokens.shape
    width = head_gain.shape[0]
    n_dp = lax.axis_size("dp")
    n_ctx = lax.axis_size("ctx")
    heads = width // HEAD_DIM
    total = features * n_dp
    columns = projections.shape[2]
    H = HEAD_DIM
    R = 16
    assert n_dp == 4 and heads == 2 and n_ctx % 2 == 0 and steps % (2 * H) == 0 and steps <= 8 * H
    vmem = pl.BlockSpec(memory_space=pltpu.VMEM)
    hbm = pl.BlockSpec(memory_space=pltpu.HBM)

    def call(kernel, arrays, outs, flops, specs=None, scratch=()):
        moved = sum(s.size * s.dtype.itemsize for s in list(arrays) + list(outs))
        return pl.pallas_call(
            kernel,
            in_specs=specs or [vmem] * len(arrays),
            out_specs=[vmem] * len(outs),
            out_shape=outs,
            scratch_shapes=list(scratch),
            compiler_params=pltpu.CompilerParams(vmem_limit_bytes=VMEM_LIMIT),
            cost_estimate=pl.CostEstimate(flops=flops, bytes_accessed=moved, transcendentals=0),
        )(*arrays)

    def arr(*shape, dtype=BF16):
        return jax.ShapeDtypeStruct(shape, dtype)

    block = 2 * steps * features * H

    def cols(bits, slot=0, n=H):
        at = (lax.axis_index("dp").astype(jnp.int32) ^ bits) * width + slot * H
        return pl.ds(pl.multiple_of(at, H), n)

    def sum_rows(ss, lanes):
        hi = ss.astype(BF16).astype(F32)
        lo = ss - hi
        row = lax.broadcasted_iota(jnp.int32, (R, lanes), 0)
        out = jnp.zeros((R, lanes), F32)
        parts = steps // lanes
        for i in range(parts):
            at = slice(i * lanes, i * lanes + lanes)
            out = jnp.where(row == i, hi[:, at], out)
            out = jnp.where(row == parts + i, lo[:, at], out)
        return out.astype(BF16)

    def read_rows(rows, lanes):
        parts = steps // lanes
        rows = rows.astype(F32)
        pieces = [rows[i:i + 1, :] + rows[parts + i:parts + i + 1, :] for i in range(parts)]
        return jnp.concatenate(pieces, axis=1)

    def first(xg, w, o0, o1):
        o0[:steps, :H] = mm(xg, w[:, cols(1, 0)]).astype(BF16)
        o0[:steps, H:] = mm(xg, w[:, cols(3, 0)]).astype(BF16)
        o1[:, :H] = mm(xg, w[:, cols(2, 1)]).astype(BF16)
        o1[:, H:] = mm(xg, w[:, cols(3, 1)]).astype(BF16)

    def first_k_kernel(x_hbm, gain_hbm, w_hbm, o0, o1, o_xg, o_w, o_sq, x, gain, sem):
        cx = pltpu.make_async_copy(x_hbm, x, sem.at[0])
        cg = pltpu.make_async_copy(gain_hbm, gain, sem.at[1])
        cw = pltpu.make_async_copy(w_hbm.at[K], o_w, sem.at[2])
        cx.start()
        cg.start()
        cw.start()
        cx.wait()
        cg.wait()
        xf = x[...].astype(F32)
        at = lax.axis_index("dp").astype(jnp.int32) * features
        g = gain[:, pl.ds(pl.multiple_of(at, H), features)]
        xg = (xf * g).astype(BF16)
        o_xg[...] = xg
        sq = xf * xf
        hi = sq.astype(BF16)
        lo = (sq - hi.astype(F32)).astype(BF16)
        ones = jnp.ones((R, features), BF16)
        dims = (((1,), (1,)), ((), ()))
        ss = lax.dot_general(ones, hi, dims, preferred_element_type=F32) + lax.dot_general(ones, lo, dims, preferred_element_type=F32)
        o_sq[...] = ss
        o0[steps:, :] = sum_rows(ss, 2 * H)
        cw.wait()
        first(xg, o_w, o0, o1)

    outs = [arr(steps + R, 2 * H), arr(steps, 2 * H), arr(steps, features), arr(features, columns), arr(R, steps, dtype=F32)]
    specs = [hbm, hbm, hbm]
    scratch = [pltpu.VMEM((steps, features), BF16), pltpu.VMEM((1, total), F32), pltpu.SemaphoreType.DMA((3,))]
    in_hbm = [pltpu.with_memory_space_constraint(a, pltpu.HBM) for a in (tokens, input_gain.reshape(1, total), projections)]
    s0, s1, xg, w_k, sq = call(first_k_kernel, in_hbm, outs, 4 * block, specs, scratch)
    k1 = swap(s0, "dp", 1), swap(s1, "dp", 2)

    def first_v_kernel(xg, w_hbm, o0, o1, o_wv, o_wq, sem):
        cv = pltpu.make_async_copy(w_hbm.at[V], o_wv, sem.at[0])
        cq = pltpu.make_async_copy(w_hbm.at[Q], o_wq, sem.at[1])
        cv.start()
        cq.start()
        cv.wait()
        first(xg[...], o_wv, o0, o1)
        cq.wait()

    outs = [arr(steps, 2 * H), arr(steps, 2 * H), arr(features, columns), arr(features, columns)]
    s0, s1, w_v, w_q = call(first_v_kernel, [xg, in_hbm[2]], outs, 4 * block, [vmem, hbm], [pltpu.SemaphoreType.DMA((2,))])
    v1 = swap(s0, "dp", 1), swap(s1, "dp", 2)

    def onward_kernel(x, wk, wv, pass_k, pass_v):
        xg = x[...]
        for w, o in ((wk, pass_k), (wv, pass_v)):
            o[:, :H] = mm(xg, w[:, cols(2, 0)])
            o[:, H:] = mm(xg, w[:, cols(1, 1)])

    pass_k, pass_v = call(onward_kernel, [xg, w_k, w_v], [arr(steps, width, dtype=F32)] * 2, 4 * block)

    def rest_kernel(x, wk, wv, wq, own_k, own_v, own_q, q1, q2, q3):
        xg = x[...]
        for bits, o in ((1, q1), (2, q2), (3, q3)):
            o[...] = mm(xg, wq[:, cols(bits, 0, width)]).astype(BF16)
        for w, own in ((wk, own_k), (wv, own_v), (wq, own_q)):
            own[...] = mm(xg, w[:, cols(0, 0, width)])

    outs = [arr(steps, width, dtype=F32)] * 3 + [arr(steps, width)] * 3
    own_k, own_v, own_q, *sends = call(rest_kernel, [xg, w_k, w_v, w_q], outs, 12 * block)

    def second_k_kernel(p, r0, r1, sq, o0, o1):
        o0[:steps, :] = (p[:, :H] + r0[:steps, H:].astype(F32)).astype(BF16)
        o1[...] = (p[:, H:] + r1[:, H:].astype(F32)).astype(BF16)
        o0[steps:, :] = sum_rows(sq[...] + read_rows(r0[steps:, :], 2 * H), H)

    s0, s1 = call(second_k_kernel, [pass_k, *k1, sq], [arr(steps + R, H), arr(steps, H)], 0)
    k2 = swap(s0, "dp", 2), swap(s1, "dp", 1)

    def second_v_kernel(p, r0, r1, o0, o1):
        o0[...] = (p[:, :H] + r0[:, H:].astype(F32)).astype(BF16)
        o1[...] = (p[:, H:] + r1[:, H:].astype(F32)).astype(BF16)

    s0, s1 = call(second_v_kernel, [pass_v, v1[0], v1[1]], [arr(steps, H), arr(steps, H)], 0)
    v2 = swap(s0, "dp", 2), swap(s1, "dp", 1)
    q_others = [swap(s, "dp", b) for b, s in zip((1, 2, 3), sends)]

    def keys_kernel(own, a0, a1, b0, b1, sq, o_k, o_s):
        ss = sq[:1, :] + read_rows(a0[steps:, :], 2 * H) + read_rows(b0[steps:, :], H)
        inv = lax.rsqrt(ss * (1.0 / total) + epsilon)
        scale = jnp.broadcast_to(inv, (H, steps)).T
        o_s[...] = scale
        for h, (a, b) in enumerate(((a0, b0), (a1, b1))):
            at = slice(h * H, h * H + H)
            u = (own[:, at] + a[:steps, :H].astype(F32) + b[:steps, :].astype(F32)) * scale
            o_k[:, at] = feature(u).astype(BF16)

    keys, scale = call(keys_kernel, [own_k, *k1, *k2, sq], [arr(steps, width), arr(steps, H, dtype=F32)], 0)

    def values_kernel(k, own, a0, a1, b0, b1, s, o_v, o_own, o_give, st):
        for h, (a, b) in enumerate(((a0, b0), (a1, b1))):
            at = slice(h * H, h * H + H)
            val = ((own[:, at] + a[:, :H].astype(F32) + b[...].astype(F32)) * s[...]).astype(BF16)
            o_v[:, at] = val
            st[h] = lax.dot_general(k[:, at], val, (((0,), (0,)), ((), ())), preferred_element_type=F32)
        odd = lax.axis_index("ctx").astype(jnp.int32) & 1
        o_own[...] = st[odd]
        o_give[...] = st[1 - odd].astype(BF16)

    outs = [arr(steps, width), arr(H, H, dtype=F32), arr(H, H)]
    scratch = [pltpu.VMEM((heads, H, H), F32)]
    values, own, give = call(values_kernel, [keys, own_v, *v1, *v2, scale], outs, 4 * steps * H * H, None, scratch)
    partner = swap(give, "ctx", 1)
    group = own + partner.astype(F32)
    before = []
    chips, span = n_ctx // 2, 1
    while span < chips:
        radix = 4 if chips % (span * 4) == 0 else 2
        sent = group.astype(BF16)
        came = [swap(sent, "ctx", 2 * span * bits) for bits in range(1, radix)]
        low = (2 * span).bit_length() - 1
        last = span * radix == chips

        def combine_kernel(*refs, low=low, radix=radix, last=last):
            first, rest = refs[:2], refs[2:]
            came, rest = rest[:radix - 1], rest[radix - 1:]
            at = lax.axis_index("ctx").astype(jnp.int32)
            digit = (at >> low) & (radix - 1)
            earlier = [((digit ^ bits) < digit).astype(jnp.int32).astype(F32) for bits in range(1, radix)]
            total_before = sum(c[...].astype(F32) * e for c, e in zip(came, earlier))
            if not last:
                out_group, out_before = rest[-2:]
                if len(rest) == 3:
                    total_before = total_before + rest[0][...]
                out_before[...] = total_before
                out_group[...] = first[0][...] + first[1][...].astype(F32) + sum(c[...].astype(F32) for c in came)
                return
            out_theirs, out_ours = rest[-2:]
            own_ref, partner_ref = rest[:2] if len(rest) >= 4 else first
            if len(rest) > 2:
                total_before = total_before + rest[-3][...]
            odd = (at & 1).astype(F32)
            out_theirs[...] = (total_before + own_ref[...] * (1.0 - odd)).astype(BF16)
            out_ours[...] = (total_before + partner_ref[...].astype(F32) * odd).astype(BF16)

        start = [own, partner] if span == 1 else [group, jnp.zeros_like(partner)]
        extra = ([own, partner] if last and span > 1 else []) + before
        outs = [arr(H, H), arr(H, H)] if last else [arr(H, H, dtype=F32)] * 2
        result = call(combine_kernel, start + came + extra, outs, 0)
        if not last:
            group, before = result[0], [result[1]]
        span *= radix
    theirs, ours = result
    other = swap(theirs, "ctx", 1)

    def inner_kernel(own, r1, r2, r3, s, k, v, o_q, o_m):
        rows = lax.broadcasted_iota(jnp.int32, (steps, steps), 0)
        causal = rows >= lax.broadcasted_iota(jnp.int32, (steps, steps), 1)
        for h in range(heads):
            at = slice(h * H, h * H + H)
            u = own[:, at] + r1[:, at].astype(F32) + r2[:, at].astype(F32) + r3[:, at].astype(F32)
            q = feature(u * s[...]).astype(BF16)
            o_q[:, at] = q
            sc = lax.dot_general(q, k[:, at], (((1,), (1,)), ((), ())), preferred_element_type=F32)
            sc = jnp.where(causal, sc, 0.0).astype(BF16)
            o_m[:, at] = mm(sc, v[:, at])

    outs = [arr(steps, width), arr(steps, width, dtype=F32)]
    queries, inner = call(inner_kernel, [own_q, *q_others, scale, keys, values], outs, 8 * steps * steps * H)

    def outer_kernel(q, inner, ours, other, hg, o):
        odd = (lax.axis_index("ctx").astype(jnp.int32) & 1) == 1
        a, b = ours[...].astype(F32), other[...].astype(F32)
        prior = jnp.where(odd, b, a).astype(BF16), jnp.where(odd, a, b).astype(BF16)
        for h in range(heads):
            at = slice(h * H, h * H + H)
            mixed = inner[:, at] + mm(q[:, at], prior[h])
            factor = lax.rsqrt(jnp.mean(mixed * mixed, axis=-1, keepdims=True) + epsilon)
            o[:, at] = (mixed * factor * hg[:, at]).astype(BF16)

    (out,) = call(outer_kernel, [queries, inner, ours, other, head_gain.reshape(1, width)], [arr(steps, width)], 4 * steps * H * H)
    return out


def solution(mesh):
    in_specs = (P("ctx", "dp"), P(), P(None, "dp", None), P("dp"))
    out_specs = P("ctx", "dp")

    return jax.shard_map(body, mesh=mesh, in_specs=in_specs, out_specs=out_specs, check_vma=False)
```

```python
import jax
import jax.numpy as jnp
from jax import lax
from jax.experimental import pallas as pl
from jax.experimental.pallas import tpu as pltpu
from jax.sharding import PartitionSpec as P

HEAD_DIM = 128
epsilon = 1e-05
F32 = jnp.float32
BF16 = jnp.bfloat16
Q, K, V = 0, 1, 2
VMEM_LIMIT = 8 * 2**20
RADIX = 4


def feature(inputs):
    return jnp.where(inputs > 0, inputs + 1.0, jnp.exp(jnp.minimum(inputs, 0.0)))


def mm(a, b):
    return jnp.dot(a, b, preferred_element_type=F32)


def swap(value, axis, bits):
    return lax.ppermute(value, axis, [(i, i ^ bits) for i in range(lax.axis_size(axis))])


def swap_by_core(value, even_bits, odd_bits):
    n_dp, n_ctx = lax.axis_size("dp"), lax.axis_size("ctx")
    pairs = []
    for i in range(n_dp):
        for j in range(n_ctx):
            other = i ^ (odd_bits if j & 1 else even_bits)
            pairs.append((i * n_ctx + j, other * n_ctx + j))
    return lax.ppermute(value, ("dp", "ctx"), pairs)


def index(axis):
    return lax.axis_index(axis).astype(jnp.int32)


def first_hop():
    return 1 + (index("ctx") & 1)


def body(tokens, input_gain, projections, head_gain):
    steps, features = tokens.shape
    width = head_gain.shape[0]
    n_dp = lax.axis_size("dp")
    n_ctx = lax.axis_size("ctx")
    heads = width // HEAD_DIM
    total = features * n_dp
    columns = projections.shape[2]
    H = HEAD_DIM
    R = 16
    assert n_dp == 4 and heads == 2 and n_ctx % 2 == 0 and features % H == 0
    assert steps == 2 * width
    vmem = pl.BlockSpec(memory_space=pltpu.VMEM)
    hbm = pl.BlockSpec(memory_space=pltpu.HBM)

    def call(kernel, arrays, outs, flops, specs=None, scratch=()):
        moved = sum(s.size * s.dtype.itemsize for s in list(arrays) + list(outs))
        return pl.pallas_call(
            kernel,
            in_specs=specs or [vmem] * len(arrays),
            out_specs=[vmem] * len(outs),
            out_shape=outs,
            scratch_shapes=list(scratch),
            compiler_params=pltpu.CompilerParams(vmem_limit_bytes=VMEM_LIMIT),
            cost_estimate=pl.CostEstimate(flops=flops, bytes_accessed=moved, transcendentals=0),
        )(*arrays)

    def arr(*shape, dtype=BF16):
        return jax.ShapeDtypeStruct(shape, dtype)

    block = 2 * steps * features * H

    def cols(bits):
        return pl.ds(pl.multiple_of((index("dp") ^ bits) * width, width), width)

    def head_cols(bits, head):
        return pl.ds(pl.multiple_of((index("dp") ^ bits) * width + head * H, H), H)

    def squares(xf):
        sq = xf * xf
        hi = sq.astype(BF16)
        lo = (sq - hi.astype(F32)).astype(BF16)
        ones = jnp.ones((R, features), BF16)
        dims = (((1,), (1,)), ((), ()))
        return lax.dot_general(ones, hi, dims, preferred_element_type=F32) + lax.dot_general(ones, lo, dims, preferred_element_type=F32)

    def sum_rows(ss, lanes):
        hi = ss.astype(BF16).astype(F32)
        lo = ss - hi
        row = lax.broadcasted_iota(jnp.int32, (R, lanes), 0)
        out = jnp.zeros((R, lanes), F32)
        parts = steps // lanes
        for i in range(parts):
            at = slice(i * lanes, i * lanes + lanes)
            out = jnp.where(row == i, hi[:, at], out)
            out = jnp.where(row == parts + i, lo[:, at], out)
        return out.astype(BF16)

    def read_rows(rows, lanes):
        parts = steps // lanes
        rows = rows.astype(F32)
        pieces = [rows[i:i + 1, :] + rows[parts + i:parts + i + 1, :] for i in range(parts)]
        return pieces[0] if parts == 1 else jnp.concatenate(pieces, axis=1)

    C = width + H

    def first_1_kernel(x_hbm, gain_hbm, w_hbm, o, o_xg, o_wk, o_wv, o_sq, x, gain, sem):
        a = first_hop()
        copies = [pltpu.make_async_copy(x_hbm, x, sem.at[0]), pltpu.make_async_copy(gain_hbm, gain, sem.at[1])]
        for i, bits in enumerate((a, 3, 3 - a, 0)):
            at = cols(bits)
            copies.append(pltpu.make_async_copy(w_hbm.at[K, :, at], o_wk.at[:, at], sem.at[2 + 2 * i]))
            copies.append(pltpu.make_async_copy(w_hbm.at[V, :, at], o_wv.at[:, at], sem.at[3 + 2 * i]))
        for c in copies:
            c.start()
        copies[0].wait()
        copies[1].wait()
        xf = x[...].astype(F32)
        g = gain[:, pl.ds(pl.multiple_of(index("dp") * features, features), features)]
        xg = (xf * g).astype(BF16)
        o_xg[...] = xg
        ss = squares(xf)
        o_sq[...] = ss
        o[steps:, :2 * width] = sum_rows(ss, 2 * width)
        o[steps:, 2 * width:] = jnp.zeros((R, 2 * C - 2 * width), BF16)
        for i, bits in enumerate((a, 3)):
            copies[2 + 2 * i].wait()
            copies[3 + 2 * i].wait()
            at = i * C
            o[:steps, at:at + width] = mm(xg, o_wk[:, cols(bits)]).astype(BF16)
            o[:steps, at + width:at + C] = mm(xg, o_wv[:, head_cols(bits, 0)]).astype(BF16)
        for c in copies[6:]:
            c.wait()

    outs = [arr(steps + R, 2 * C), arr(steps, features), arr(features, columns), arr(features, columns), arr(R, steps, dtype=F32)]
    scratch = [pltpu.VMEM((steps, features), BF16), pltpu.VMEM((1, total), F32), pltpu.SemaphoreType.DMA((10,))]
    in_hbm = [pltpu.with_memory_space_constraint(a, pltpu.HBM) for a in (tokens, input_gain.reshape(1, total), projections)]
    s0, xg, w_k, w_v, sq = call(first_1_kernel, in_hbm, outs, 6 * block, [hbm] * 3, scratch)
    a1 = swap_by_core(s0, 1, 2)

    def first_2_kernel(x, wv, w_hbm, o, o_wq, sem):
        cq = pltpu.make_async_copy(w_hbm.at[Q], o_wq, sem.at[0])
        cq.start()
        xg = x[...]
        o[:, :H] = mm(xg, wv[:, head_cols(first_hop(), 1)]).astype(BF16)
        o[:, H:] = mm(xg, wv[:, head_cols(3, 1)]).astype(BF16)
        cq.wait()

    outs = [arr(steps, 2 * H), arr(features, columns)]
    s0, w_q = call(first_2_kernel, [xg, w_v, in_hbm[2]], outs, 2 * block, [vmem, vmem, hbm], [pltpu.SemaphoreType.DMA((1,))])
    b1 = swap_by_core(s0, 1, 2)

    def onward_kernel(x, wk, wv, pass_a, pass_b):
        xg = x[...]
        bits = 3 - first_hop()
        pass_a[:, :width] = mm(xg, wk[:, cols(bits)])
        v = mm(xg, wv[:, cols(bits)])
        pass_a[:, width:] = v[:, :H]
        pass_b[...] = v[:, H:]

    outs = [arr(steps, C, dtype=F32), arr(steps, H, dtype=F32)]
    pass_a, pass_b = call(onward_kernel, [xg, w_k, w_v], outs, 4 * block)

    def rest_kernel(x, wk, wv, wq, own_k, own_v, own_q, q1, q2, q3):
        xg = x[...]
        for bits, o in ((3 - first_hop(), q1), (first_hop(), q2), (3, q3)):
            o[...] = mm(xg, wq[:, cols(bits)]).astype(BF16)
        for w, own in ((wk, own_k), (wv, own_v), (wq, own_q)):
            own[...] = mm(xg, w[:, cols(0)])

    outs = [arr(steps, width, dtype=F32)] * 3 + [arr(steps, width)] * 3
    own_k, own_v, own_q, *sends = call(rest_kernel, [xg, w_k, w_v, w_q], outs, 12 * block)

    def second_1_kernel(p, r, sq, o):
        o[:steps, :] = (p[...] + r[:steps, C:].astype(F32)).astype(BF16)
        o[steps:, :width] = sum_rows(sq[...] + read_rows(r[steps:, :2 * width], 2 * width), width)
        o[steps:, width:] = jnp.zeros((R, H), BF16)

    (s0,) = call(second_1_kernel, [pass_a, a1, sq], [arr(steps + R, C)], 0)
    a2 = swap_by_core(s0, 2, 1)

    def second_2_kernel(p, r, o):
        o[...] = (p[...] + r[:, H:].astype(F32)).astype(BF16)

    (s0,) = call(second_2_kernel, [pass_b, b1], [arr(steps, H)], 0)
    b2 = swap_by_core(s0, 2, 1)
    q_others = [swap_by_core(sends[0], 2, 1), swap_by_core(sends[1], 1, 2), swap(sends[2], "dp", 3)]

    def state_of(k, v):
        return lax.dot_general(k, v, (((0,), (0,)), ((), ())), preferred_element_type=F32)

    def keys_kernel(own_k, own_v, a, b, sq, o_k, o_v, o_s, o_st):
        ss = sq[:1, :] + read_rows(a[steps:, :2 * width], 2 * width) + read_rows(b[steps:, :width], width)
        inv = lax.rsqrt(ss * (1.0 / total) + epsilon)
        scale = jnp.broadcast_to(inv, (H, steps)).T
        o_s[...] = scale
        for h in range(heads):
            at = slice(h * H, h * H + H)
            u = (own_k[:, at] + a[:steps, at].astype(F32) + b[:steps, at].astype(F32)) * scale
            o_k[:, at] = feature(u).astype(BF16)
        at = slice(width, C)
        val = ((own_v[:, :H] + a[:steps, at].astype(F32) + b[:steps, at].astype(F32)) * scale).astype(BF16)
        o_v[...] = val
        o_st[...] = state_of(o_k[:, :H], val)

    outs = [arr(steps, width), arr(steps, H), arr(steps, H, dtype=F32), arr(H, H, dtype=F32)]
    keys, values_0, scale, state_0 = call(keys_kernel, [own_k, own_v, a1, a2, sq], outs, 2 * steps * H * H)

    def values_kernel(k, own, a, b, s, st0, o_v, o_own, o_give):
        val = ((own[:, H:] + a[:, :H].astype(F32) + b[...].astype(F32)) * s[...]).astype(BF16)
        o_v[...] = val
        st1 = state_of(k[:, H:], val)
        odd = (index("ctx") & 1) == 1
        o_own[...] = jnp.where(odd, st1, st0[...])
        o_give[...] = jnp.where(odd, st0[...], st1).astype(BF16)

    outs = [arr(steps, H), arr(H, H, dtype=F32), arr(H, H)]
    values_1, own, give = call(values_kernel, [keys, own_v, b1, b2, scale, state_0], outs, 2 * steps * H * H)
    partner = swap(give, "ctx", 1)
    group = own + partner.astype(F32)
    before = []
    chips, span = n_ctx // 2, 1
    while span < chips:
        radix = RADIX if chips % (span * RADIX) == 0 else 2
        sent = group.astype(BF16)
        came = [swap(sent, "ctx", 2 * span * bits) for bits in range(1, radix)]
        low = (2 * span).bit_length() - 1
        last = span * radix == chips

        def combine_kernel(*refs, low=low, radix=radix, last=last):
            first, rest = refs[:2], refs[2:]
            came, rest = rest[:radix - 1], rest[radix - 1:]
            at = index("ctx")
            digit = (at >> low) & (radix - 1)
            earlier = [((digit ^ bits) < digit).astype(jnp.int32).astype(F32) for bits in range(1, radix)]
            total_before = sum(c[...].astype(F32) * e for c, e in zip(came, earlier))
            if not last:
                out_group, out_before = rest[-2:]
                if len(rest) == 3:
                    total_before = total_before + rest[0][...]
                out_before[...] = total_before
                out_group[...] = first[0][...] + first[1][...].astype(F32) + sum(c[...].astype(F32) for c in came)
                return
            out_theirs, out_ours = rest[-2:]
            own_ref, partner_ref = rest[:2] if len(rest) >= 4 else first
            if len(rest) > 2:
                total_before = total_before + rest[-3][...]
            odd = (at & 1).astype(F32)
            out_theirs[...] = (total_before + own_ref[...] * (1.0 - odd)).astype(BF16)
            out_ours[...] = (total_before + partner_ref[...].astype(F32) * odd).astype(BF16)

        start = [own, partner] if span == 1 else [group, jnp.zeros_like(partner)]
        extra = ([own, partner] if last and span > 1 else []) + before
        outs = [arr(H, H), arr(H, H)] if last else [arr(H, H, dtype=F32)] * 2
        result = call(combine_kernel, start + came + extra, outs, 0)
        if not last:
            group, before = result[0], [result[1]]
        span *= radix
    theirs, ours = result
    other = swap(theirs, "ctx", 1)

    def inner_kernel(own, r1, r2, r3, s, k, v0, v1, o_q, o_m):
        rows = lax.broadcasted_iota(jnp.int32, (steps, steps), 0)
        causal = rows >= lax.broadcasted_iota(jnp.int32, (steps, steps), 1)
        for h, v in enumerate((v0, v1)):
            at = slice(h * H, h * H + H)
            u = own[:, at] + r1[:, at].astype(F32) + r2[:, at].astype(F32) + r3[:, at].astype(F32)
            q = feature(u * s[...]).astype(BF16)
            o_q[:, at] = q
            sc = lax.dot_general(q, k[:, at], (((1,), (1,)), ((), ())), preferred_element_type=F32)
            sc = jnp.where(causal, sc, 0.0).astype(BF16)
            o_m[:, at] = mm(sc, v[...])

    outs = [arr(steps, width), arr(steps, width, dtype=F32)]
    queries, inner = call(inner_kernel, [own_q, *q_others, scale, keys, values_0, values_1], outs, 8 * steps * steps * H)

    def outer_kernel(q, inner, ours, other, hg, o):
        odd = (index("ctx") & 1) == 1
        a, b = ours[...].astype(F32), other[...].astype(F32)
        prior = jnp.where(odd, b, a).astype(BF16), jnp.where(odd, a, b).astype(BF16)
        for h in range(heads):
            at = slice(h * H, h * H + H)
            mixed = inner[:, at] + mm(q[:, at], prior[h])
            factor = lax.rsqrt(jnp.mean(mixed * mixed, axis=-1, keepdims=True) + epsilon)
            o[:, at] = (mixed * factor * hg[:, at]).astype(BF16)

    (out,) = call(outer_kernel, [queries, inner, ours, other, head_gain.reshape(1, width)], [arr(steps, width)], 4 * steps * H * H)
    return out


def solution(mesh):
    in_specs = (P("ctx", "dp"), P(), P(None, "dp", None), P("dp"))
    out_specs = P("ctx", "dp")

    return jax.shard_map(body, mesh=mesh, in_specs=in_specs, out_specs=out_specs, check_vma=False)
```

```python
import jax
import jax.numpy as jnp
from jax import lax
from jax.experimental import pallas as pl
from jax.experimental.pallas import tpu as pltpu
from jax.sharding import PartitionSpec as P

HEAD_DIM = 128
epsilon = 1e-05
F32 = jnp.float32
BF16 = jnp.bfloat16
Q, K, V = 0, 1, 2
VMEM_LIMIT = 8 * 2**20
RADIX = 4


def feature(inputs):
    return jnp.where(inputs > 0, inputs + 1.0, jnp.exp(jnp.minimum(inputs, 0.0)))


def mm(a, b):
    return jnp.dot(a, b, preferred_element_type=F32)


def swap(value, axis, bits):
    return lax.ppermute(value, axis, [(i, i ^ bits) for i in range(lax.axis_size(axis))])


def swap_by_core(value, even_bits, odd_bits):
    n_dp, n_ctx = lax.axis_size("dp"), lax.axis_size("ctx")
    pairs = []
    for i in range(n_dp):
        for j in range(n_ctx):
            other = i ^ (odd_bits if j & 1 else even_bits)
            pairs.append((i * n_ctx + j, other * n_ctx + j))
    return lax.ppermute(value, ("dp", "ctx"), pairs)


def index(axis):
    return lax.axis_index(axis).astype(jnp.int32)


def first_hop():
    return 1 + (index("ctx") & 1)


def body(tokens, input_gain, projections, head_gain):
    steps, features = tokens.shape
    width = head_gain.shape[0]
    n_dp = lax.axis_size("dp")
    n_ctx = lax.axis_size("ctx")
    heads = width // HEAD_DIM
    total = features * n_dp
    columns = projections.shape[2]
    H = HEAD_DIM
    R = 16
    assert n_dp == 4 and heads == 2 and n_ctx % 2 == 0 and features % H == 0
    assert steps == 2 * width
    vmem = pl.BlockSpec(memory_space=pltpu.VMEM)
    hbm = pl.BlockSpec(memory_space=pltpu.HBM)

    def call(kernel, arrays, outs, flops, specs=None, scratch=()):
        moved = sum(s.size * s.dtype.itemsize for s in list(arrays) + list(outs))
        return pl.pallas_call(
            kernel,
            in_specs=specs or [vmem] * len(arrays),
            out_specs=[vmem] * len(outs),
            out_shape=outs,
            scratch_shapes=list(scratch),
            compiler_params=pltpu.CompilerParams(vmem_limit_bytes=VMEM_LIMIT),
            cost_estimate=pl.CostEstimate(flops=flops, bytes_accessed=moved, transcendentals=0),
        )(*arrays)

    def arr(*shape, dtype=BF16):
        return jax.ShapeDtypeStruct(shape, dtype)

    block = 2 * steps * features * H

    def cols(bits):
        return pl.ds(pl.multiple_of((index("dp") ^ bits) * width, width), width)

    def squares(xf):
        sq = xf * xf
        hi = sq.astype(BF16)
        lo = (sq - hi.astype(F32)).astype(BF16)
        ones = jnp.ones((R, features), BF16)
        dims = (((1,), (1,)), ((), ()))
        return lax.dot_general(ones, hi, dims, preferred_element_type=F32) + lax.dot_general(ones, lo, dims, preferred_element_type=F32)

    def sum_rows(ss, lanes):
        hi = ss.astype(BF16).astype(F32)
        lo = ss - hi
        row = lax.broadcasted_iota(jnp.int32, (R, lanes), 0)
        out = jnp.zeros((R, lanes), F32)
        parts = steps // lanes
        for i in range(parts):
            at = slice(i * lanes, i * lanes + lanes)
            out = jnp.where(row == i, hi[:, at], out)
            out = jnp.where(row == parts + i, lo[:, at], out)
        return out.astype(BF16)

    def read_rows(rows, lanes):
        parts = steps // lanes
        rows = rows.astype(F32)
        pieces = [rows[i:i + 1, :] + rows[parts + i:parts + i + 1, :] for i in range(parts)]
        return pieces[0] if parts == 1 else jnp.concatenate(pieces, axis=1)

    C = width + H

    def first_k_kernel(x_hbm, gain_hbm, w_hbm, o, o_xg, x, gain, w, sem):
        copies = [pltpu.make_async_copy(x_hbm, x, sem.at[0]), pltpu.make_async_copy(gain_hbm, gain, sem.at[1])]
        for i, bits in enumerate((first_hop(), 3)):
            copies.append(pltpu.make_async_copy(w_hbm.at[K, :, cols(bits)], w.at[i], sem.at[2 + i]))
        for c in copies:
            c.start()
        copies[0].wait()
        copies[1].wait()
        g = gain[:, pl.ds(pl.multiple_of(index("dp") * features, features), features)]
        xg = (x[...].astype(F32) * g).astype(BF16)
        o_xg[...] = xg
        for i in range(2):
            copies[2 + i].wait()
            o[:, i * width:i * width + width] = mm(xg, w[i]).astype(BF16)

    outs = [arr(steps, 2 * width), arr(steps, features)]
    scratch = [pltpu.VMEM((steps, features), BF16), pltpu.VMEM((1, total), F32), pltpu.VMEM((2, features, width), BF16), pltpu.SemaphoreType.DMA((4,))]
    in_hbm = [pltpu.with_memory_space_constraint(a, pltpu.HBM) for a in (tokens, input_gain.reshape(1, total), projections)]
    s0, xg = call(first_k_kernel, in_hbm, outs, 4 * block, [hbm] * 3, scratch)
    ka1 = swap_by_core(s0, 1, 2)

    def first_v_kernel(xg_ref, x_hbm, w_hbm, o0, o1, o_wk, o_wv, o_wq, o_sq, x, sem):
        copies = [pltpu.make_async_copy(x_hbm, x, sem.at[3])]
        copies += [pltpu.make_async_copy(w_hbm.at[p], o, sem.at[i]) for i, (p, o) in enumerate(((V, o_wv), (K, o_wk), (Q, o_wq)))]
        for c in copies:
            c.start()
        copies[0].wait()
        ss = squares(x[...].astype(F32))
        o_sq[...] = ss
        o0[steps:, :] = sum_rows(ss, 2 * H)
        copies[1].wait()
        xg = xg_ref[...]
        for i, bits in enumerate((first_hop(), 3)):
            v = mm(xg, o_wv[:, cols(bits)]).astype(BF16)
            o0[:steps, i * H:i * H + H] = v[:, :H]
            o1[:, i * H:i * H + H] = v[:, H:]
        copies[2].wait()
        copies[3].wait()

    outs = [arr(steps + R, 2 * H), arr(steps, 2 * H)] + [arr(features, columns)] * 3 + [arr(R, steps, dtype=F32)]
    scratch = [pltpu.VMEM((steps, features), BF16), pltpu.SemaphoreType.DMA((4,))]
    s0, s1, w_k, w_v, w_q, sq = call(first_v_kernel, [xg, in_hbm[0], in_hbm[2]], outs, 4 * block, [vmem, hbm, hbm], scratch)
    va1 = swap_by_core(s0, 1, 2)
    b1 = swap_by_core(s1, 1, 2)

    def onward_kernel(x, wk, wv, pass_a, pass_b):
        xg = x[...]
        bits = 3 - first_hop()
        pass_a[:, :width] = mm(xg, wk[:, cols(bits)])
        v = mm(xg, wv[:, cols(bits)])
        pass_a[:, width:] = v[:, :H]
        pass_b[...] = v[:, H:]

    outs = [arr(steps, C, dtype=F32), arr(steps, H, dtype=F32)]
    pass_a, pass_b = call(onward_kernel, [xg, w_k, w_v], outs, 4 * block)

    def rest_kernel(x, wk, wv, wq, own_k, own_v, own_q, q1, q2, q3):
        xg = x[...]
        for bits, o in ((3 - first_hop(), q1), (first_hop(), q2), (3, q3)):
            o[...] = mm(xg, wq[:, cols(bits)]).astype(BF16)
        for w, own in ((wk, own_k), (wv, own_v), (wq, own_q)):
            own[...] = mm(xg, w[:, cols(0)])

    outs = [arr(steps, width, dtype=F32)] * 3 + [arr(steps, width)] * 3
    own_k, own_v, own_q, *sends = call(rest_kernel, [xg, w_k, w_v, w_q], outs, 12 * block)

    def second_1_kernel(p, r, rv, sq, o):
        o[:steps, :width] = (p[:, :width] + r[:, width:].astype(F32)).astype(BF16)
        o[:steps, width:] = (p[:, width:] + rv[:steps, H:].astype(F32)).astype(BF16)
        o[steps:, :width] = sum_rows(sq[...] + read_rows(rv[steps:, :], 2 * H), width)
        o[steps:, width:] = jnp.zeros((R, H), BF16)

    (s0,) = call(second_1_kernel, [pass_a, ka1, va1, sq], [arr(steps + R, C)], 0)
    a2 = swap_by_core(s0, 2, 1)

    def second_2_kernel(p, r, o):
        o[...] = (p[...] + r[:, H:].astype(F32)).astype(BF16)

    (s0,) = call(second_2_kernel, [pass_b, b1], [arr(steps, H)], 0)
    b2 = swap_by_core(s0, 2, 1)
    q_others = [swap_by_core(sends[0], 2, 1), swap_by_core(sends[1], 1, 2), swap(sends[2], "dp", 3)]

    def state_of(k, v):
        return lax.dot_general(k, v, (((0,), (0,)), ((), ())), preferred_element_type=F32)

    def keys_kernel(own_k, own_v, a, va, b, sq, o_k, o_v, o_s, o_st):
        ss = sq[:1, :] + read_rows(va[steps:, :], 2 * H) + read_rows(b[steps:, :width], width)
        inv = lax.rsqrt(ss * (1.0 / total) + epsilon)
        scale = jnp.broadcast_to(inv, (H, steps)).T
        o_s[...] = scale
        for h in range(heads):
            at = slice(h * H, h * H + H)
            u = (own_k[:, at] + a[:, at].astype(F32) + b[:steps, at].astype(F32)) * scale
            o_k[:, at] = feature(u).astype(BF16)
        val = ((own_v[:, :H] + va[:steps, :H].astype(F32) + b[:steps, width:].astype(F32)) * scale).astype(BF16)
        o_v[...] = val
        o_st[...] = state_of(o_k[:, :H], val)

    outs = [arr(steps, width), arr(steps, H), arr(steps, H, dtype=F32), arr(H, H, dtype=F32)]
    keys, values_0, scale, state_0 = call(keys_kernel, [own_k, own_v, ka1, va1, a2, sq], outs, 2 * steps * H * H)

    def values_kernel(k, own, a, b, s, st0, o_v, o_own, o_give):
        val = ((own[:, H:] + a[:, :H].astype(F32) + b[...].astype(F32)) * s[...]).astype(BF16)
        o_v[...] = val
        st1 = state_of(k[:, H:], val)
        odd = (index("ctx") & 1) == 1
        o_own[...] = jnp.where(odd, st1, st0[...])
        o_give[...] = jnp.where(odd, st0[...], st1).astype(BF16)

    outs = [arr(steps, H), arr(H, H, dtype=F32), arr(H, H)]
    values_1, own, give = call(values_kernel, [keys, own_v, b1, b2, scale, state_0], outs, 2 * steps * H * H)
    partner = swap(give, "ctx", 1)
    group = own + partner.astype(F32)
    before = []
    chips, span = n_ctx // 2, 1
    while span < chips:
        radix = RADIX if chips % (span * RADIX) == 0 else 2
        sent = group.astype(BF16)
        came = [swap(sent, "ctx", 2 * span * bits) for bits in range(1, radix)]
        low = (2 * span).bit_length() - 1
        last = span * radix == chips

        def combine_kernel(*refs, low=low, radix=radix, last=last):
            first, rest = refs[:2], refs[2:]
            came, rest = rest[:radix - 1], rest[radix - 1:]
            at = index("ctx")
            digit = (at >> low) & (radix - 1)
            earlier = [((digit ^ bits) < digit).astype(jnp.int32).astype(F32) for bits in range(1, radix)]
            total_before = sum(c[...].astype(F32) * e for c, e in zip(came, earlier))
            if not last:
                out_group, out_before = rest[-2:]
                if len(rest) == 3:
                    total_before = total_before + rest[0][...]
                out_before[...] = total_before
                out_group[...] = first[0][...] + first[1][...].astype(F32) + sum(c[...].astype(F32) for c in came)
                return
            out_theirs, out_ours = rest[-2:]
            own_ref, partner_ref = rest[:2] if len(rest) >= 4 else first
            if len(rest) > 2:
                total_before = total_before + rest[-3][...]
            odd = (at & 1).astype(F32)
            out_theirs[...] = (total_before + own_ref[...] * (1.0 - odd)).astype(BF16)
            out_ours[...] = (total_before + partner_ref[...].astype(F32) * odd).astype(BF16)

        start = [own, partner] if span == 1 else [group, jnp.zeros_like(partner)]
        extra = ([own, partner] if last and span > 1 else []) + before
        outs = [arr(H, H), arr(H, H)] if last else [arr(H, H, dtype=F32)] * 2
        result = call(combine_kernel, start + came + extra, outs, 0)
        if not last:
            group, before = result[0], [result[1]]
        span *= radix
    theirs, ours = result
    other = swap(theirs, "ctx", 1)

    def inner_kernel(own, r1, r2, r3, s, k, v0, v1, o_q, o_m):
        rows = lax.broadcasted_iota(jnp.int32, (steps, steps), 0)
        causal = rows >= lax.broadcasted_iota(jnp.int32, (steps, steps), 1)
        for h, v in enumerate((v0, v1)):
            at = slice(h * H, h * H + H)
            u = own[:, at] + r1[:, at].astype(F32) + r2[:, at].astype(F32) + r3[:, at].astype(F32)
            q = feature(u * s[...]).astype(BF16)
            o_q[:, at] = q
            sc = lax.dot_general(q, k[:, at], (((1,), (1,)), ((), ())), preferred_element_type=F32)
            sc = jnp.where(causal, sc, 0.0).astype(BF16)
            o_m[:, at] = mm(sc, v[...])

    outs = [arr(steps, width), arr(steps, width, dtype=F32)]
    queries, inner = call(inner_kernel, [own_q, *q_others, scale, keys, values_0, values_1], outs, 8 * steps * steps * H)

    def outer_kernel(q, inner, ours, other, hg, o):
        odd = (index("ctx") & 1) == 1
        a, b = ours[...].astype(F32), other[...].astype(F32)
        prior = jnp.where(odd, b, a).astype(BF16), jnp.where(odd, a, b).astype(BF16)
        for h in range(heads):
            at = slice(h * H, h * H + H)
            mixed = inner[:, at] + mm(q[:, at], prior[h])
            factor = lax.rsqrt(jnp.mean(mixed * mixed, axis=-1, keepdims=True) + epsilon)
            o[:, at] = (mixed * factor * hg[:, at]).astype(BF16)

    (out,) = call(outer_kernel, [queries, inner, ours, other, head_gain.reshape(1, width)], [arr(steps, width)], 4 * steps * H * H)
    return out


def solution(mesh):
    in_specs = (P("ctx", "dp"), P(), P(None, "dp", None), P("dp"))
    out_specs = P("ctx", "dp")

    return jax.shard_map(body, mesh=mesh, in_specs=in_specs, out_specs=out_specs, check_vma=False)
```
